32 devices in a mesh: row: 4 (over y, x), col: 8 (over z, core).
Axes of the slice: x: 2, y: 2, z: 4, core: 2. Of those that a mesh axis runs over, the one named last changes fastest.
Arguments:
- feat_rows: float32 [2048, 512], P(('row', 'col')), may hold values from -0.6 to 0.6
- feat_cols: float32 [2048, 512], P(('col', 'row')), may hold values from -0.6 to 0.6
- panel_rows: float32 [2048, 1024], P(('row', 'col')), may hold values from -0.6 to 0.6
- panel_cols: float32 [2048, 1024], P(('col', 'row')), may hold values from -0.6 to 0.6
- accumulator: float32 [2048, 2048], P('row', 'col'), may hold values from -1.8 to 1.8
Outputs:
- acc_new: float32 [2048, 2048], P('row', 'col')
- grad_rows: float32 [2048, 512], P(('row', 'col'))
- grad_cols: float32 [2048, 512], P(('col', 'row'))
The draws below stay inside these ranges and needn't reach their ends.
All inputs are finite; a program needn't handle non-finite values.
Results may differ from the reference program's by a relative error of at most 0.00011.
Values sent between devices are 32-bit elements; how exact they have to be, the bound alone decides.
A program may use at most 64 MiB of HBM per device.

```python
import jax
import jax.numpy as jnp
from jax import lax

F = 512
PANEL = 512
PANELS = 2
NA = 2048
NB = 2048
N_ROW = 4


def steps_of(key, extent, pieces, least, top_value):
    factor_of, own = 1.0, jax.random.fold_in(key, 6)
    for position, parts in pieces:
        heights = jnp.exp(jax.random.uniform(jax.random.fold_in(own, position), (parts,), jnp.float32, least / len(pieces), top_value / len(pieces)))
        factor_of = factor_of * jnp.repeat(heights, extent[position] // parts).reshape([-1 if axis == position else 1 for axis in range(len(extent))])
    return factor_of


def scatter_about(rng, extent, scale, limit, split=(), kind=jnp.bfloat16):
    gain = steps_of(rng, extent, split, -0.22, 0.18) if split else 1.0
    result = jax.random.normal(rng, extent, jnp.float32) * scale * gain
    return jnp.minimum(jnp.maximum(result, -limit), limit).astype(kind)


def setup_inputs(seed: int = 0) -> dict:
    streams_of = jax.random.split(jax.random.key(seed), 6)
    return {
        "feat_rows": scatter_about(streams_of[0], (NA, F), 0.1, 0.6, ((0, 32),), jnp.float32),
        "feat_cols": scatter_about(streams_of[1], (NB, F), 0.1, 0.6, ((0, 32),), jnp.float32),
        "panel_rows": scatter_about(streams_of[2], (NA, PANELS * PANEL), 0.1, 0.6, ((0, 32),), jnp.float32),
        "panel_cols": scatter_about(streams_of[3], (NB, PANELS * PANEL), 0.1, 0.6, ((0, 32),), jnp.float32),
        "accumulator": scatter_about(streams_of[4], (NA, NB), 0.3, 1.8, ((0, 4), (1, 8)), jnp.float32),
    }


decay_rate = 0.125
grad_scale = 0.25


def local_tile(rows_feat, rows_panel, acc_tile, cols_feat, cols_panel):
    grams_tile = acc_tile + jnp.dot(rows_panel, cols_panel.T, precision=lax.Precision.HIGHEST)
    cross_term = jnp.dot(rows_feat, cols_feat.T, precision=lax.Precision.HIGHEST)
    norm_rows = jnp.sum(rows_feat * rows_feat, axis=1)
    norm_cols = jnp.sum(cols_feat * cols_feat, axis=1)
    dist_sq = norm_rows[:, None] + norm_cols[None, :] - 2.0 * cross_term
    kernel = jnp.exp(-decay_rate * dist_sq)
    weights = grams_tile * kernel
    row_term = grad_scale * (jnp.dot(weights, cols_feat, precision=lax.Precision.HIGHEST) - jnp.sum(weights, axis=1)[:, None] * rows_feat)
    col_term = grad_scale * (jnp.dot(weights.T, rows_feat, precision=lax.Precision.HIGHEST) - jnp.sum(weights, axis=0)[:, None] * cols_feat)
    return grams_tile, row_term, col_term


def reference(feat_rows, feat_cols, panel_rows, panel_cols, accumulator):
    blocks = N_ROW
    height = NA // blocks
    rows_feat = feat_rows.reshape(blocks, height, F)
    rows_panel = panel_rows.reshape(blocks, height, PANELS * PANEL)
    acc_blocks = accumulator.reshape(blocks, height, NB)

    def step_fn(totals, inputs):
        feat_blk, panel_blk, acc_blk = inputs
        grams_tile, row_term, col_term = local_tile(feat_blk, panel_blk, acc_blk, feat_cols, panel_cols)
        return totals + col_term, (grams_tile, row_term)

    init = jnp.zeros((NB, F), jnp.float32)
    col_total, outputs = lax.scan(step_fn, init, (rows_feat, rows_panel, acc_blocks))
    acc_new = outputs[0].reshape(NA, NB)
    grad_rows = outputs[1].reshape(NA, F)
    return acc_new, grad_rows, col_total
```

```python
import functools

import jax
import jax.numpy as jnp
from jax import lax
from jax.experimental import pallas as pl
from jax.experimental.pallas import tpu as pltpu
from jax.sharding import PartitionSpec as P

decay_rate = 0.125
grad_scale = 0.25
MESH = pl.DeviceIdType.MESH
HALVES = 2
LEAD = 2


def split(x):
    hi = x.astype(jnp.bfloat16)
    return hi, (x - hi.astype(jnp.float32)).astype(jnp.bfloat16)


def dot3(a, b, ca, cb):
    dims = (((ca,), (cb,)), ((), ()))
    f = functools.partial(lax.dot_general, dimension_numbers=dims, preferred_element_type=jnp.float32)
    return f(a[0], b[0]) + (f(a[0], b[1]) + f(a[1], b[0]))


def order(n, depth, y, t):
    src, chunk = y * 0, t * 0
    found = y < 0
    for _ in range(depth):
        lead = t < LEAD
        done = jnp.logical_or(lead, t >= LEAD + n * y)
        take = jnp.logical_and(done, jnp.logical_not(found))
        src = jnp.where(take, y, src)
        chunk = jnp.where(take, jnp.where(lead, t, t - n * y), chunk)
        found = jnp.logical_or(found, done)
        y, t = y - 1, t - LEAD
    return src, chunk


def done_slot(n, depth, z, s):
    def seq(y):
        if y == 0:
            return [(0, i) for i in range(n)]
        own = [(y, i) for i in range(n)]
        return own[:LEAD] + seq(y - 1) + own[LEAD:]

    if s == z:
        return -1
    y, ys = (z, s) if s < z else (depth - 1 - z, depth - 1 - s)
    return max(t for t, (a, _) in enumerate(seq(y - 1)) if a == ys)


def plan(n, depth):
    table, need = [], [0] * depth
    for z in range(depth):
        shards = sorted(range(depth), key=lambda s: (done_slot(n, depth, z, s), -abs(s - z)))
        far = [s for s in shards if s != z]
        if z in (0, depth - 1):
            far.insert(len(far) - 1, z)
        else:
            far = sorted(far, key=lambda s: (-abs(s - z), s < z)) + [z]
        table.append(far)
        for j, s in enumerate(far):
            need[j] = max(need[j], done_slot(n, depth, z, s) + 1)
    for j in range(1, depth):
        need[j] = max(need[j], need[j - 1])
    need[0] = max(need[0], n * (depth - 2))
    for j in range(1, depth):
        need[j] = max(need[j], need[0])
    need[-1] = max(need[-1], n * (depth - 1))
    return table, need


def pick(values, at):
    out = jnp.int32(values[0])
    for i, v in enumerate(values[1:], 1):
        out = jnp.where(at == i, jnp.int32(v), out)
    return out


def kernel(R, C, fr, fc, pr, pc, acc, acc_out, gr_out, gc_out,
           rows, cols, chi, clo, ncol, accv, rowp, sibp, chbuf, sumb, colacc, tacc, colr,
           lsem, osem, rrecv, zss, sss, css, crecv, rss, rsr, chs, chrecv, gcs, gcr):
    me_r, me_c = lax.axis_index("row"), lax.axis_index("col")
    z, k = me_c // 2, me_c % 2
    Z = C // 2
    NR, F = fr.shape
    NC = fc.shape[0]
    Q = 1 + pr.shape[1] // F
    n = HALVES * Q
    hr = NR // HALVES
    sibling = (me_r, me_c + 1 - 2 * k)
    place = (z, Z - 1 - z)
    step_to = (2, -2)
    table, need = plan(n, Z)

    def at(start, size, mult):
        return pl.ds(pl.multiple_of(start, mult), size)

    def rchunk(c, i):
        return rows.at[i % Q, at(c * NR + (i // Q) * hr, hr, 8), :]

    def remote(src, dst, ss, rs, dev):
        return pltpu.make_async_remote_copy(src_ref=src, dst_ref=dst, send_sem=ss, recv_sem=rs, device_id=dev, device_id_type=MESH)

    def zcopy(d, zs, i):
        c = 2 * zs + k
        return remote(rchunk(c, i), rchunk(c, i), zss.at[d, zs, i], rrecv.at[c, i], (me_r, me_c + step_to[d]))

    def scopy(zs, core, i):
        c = 2 * zs + core
        return remote(rchunk(c, i), rchunk(c, i), sss.at[zs, i], rrecv.at[c, i], sibling)

    local = []
    for q in range(Q):
        rsrc = fr if q == 0 else pr.at[:, pl.ds((q - 1) * F, F)]
        csrc = fc if q == 0 else pc.at[:, pl.ds((q - 1) * F, F)]
        local.append(pltpu.make_async_copy(rsrc, rows.at[q, at(me_c * NR, NR, 8), :], lsem.at[2 * q]))
        local.append(pltpu.make_async_copy(csrc, cols.at[q, at(me_r * NC, NC, 8), :], lsem.at[2 * q + 1]))
    acc_in = pltpu.make_async_copy(acc, accv, lsem.at[2 * Q])
    for copy in local:
        copy.start()
    acc_in.start()

    barrier = pltpu.get_barrier_semaphore()

    def greet(p, carry):
        pl.semaphore_signal(barrier, inc=1, device_id=((me_r + p) % R, me_c), device_id_type=MESH)
        return carry

    lax.fori_loop(1, R, greet, 0)
    pl.semaphore_signal(barrier, inc=1, device_id=sibling, device_id_type=MESH)
    for d in range(2):
        @pl.when(place[d] < Z - 1)
        def _():
            pl.semaphore_signal(barrier, inc=1, device_id=(me_r, me_c + step_to[d]), device_id_type=MESH)
    for copy in local:
        copy.wait()
    pl.semaphore_wait(barrier, R + (z > 0).astype(jnp.int32) + (z < Z - 1).astype(jnp.int32))

    for d in range(2):
        @pl.when(place[d] < Z - 1)
        def _():
            for i in range(LEAD):
                zcopy(d, z, i).start()

    def col_send(p, q):
        block = cols.at[q, at(me_r * NC, NC, 8), :]
        return remote(block, block, css.at[p, q], crecv.at[me_r, q], ((me_r + p) % R, me_c))

    def col_recv(p, q):
        src = (me_r + p) % R
        block = cols.at[q, at(src * NC, NC, 8), :]
        return remote(block, block, css.at[p, q], crecv.at[src, q], ((me_r + p) % R, me_c))

    def push_cols(p, carry):
        for q in range(Q):
            col_send(p, q).start()
        return carry

    lax.fori_loop(1, R, push_cols, 0)
    for d in range(2):
        @pl.when(place[d] == 0)
        def _():
            for i in range(LEAD, n):
                zcopy(d, z, i).start()
    for i in range(n):
        scopy(z, k, i).start()

    def slot(t, carry):
        for d in range(2):
            y = place[d]

            @pl.when(t < n * y)
            def _():
                ys, i = order(n, Z, y - 1, t)
                zs = ys if d == 0 else Z - 1 - ys
                zcopy(d, zs, i).wait_recv()

                @pl.when(y < Z - 1)
                def _():
                    zcopy(d, zs, i).start()

                scopy(zs, k, i).start()

                @pl.when(jnp.logical_and(t == n * y - 1, y < Z - 1))
                def _():
                    for j in range(LEAD, n):
                        zcopy(d, z, j).start()

        return carry

    lax.fori_loop(0, need[0], slot, 0)

    def await_cols(p, carry):
        for q in range(Q):
            col_recv(p, q).wait_recv()
        return carry

    lax.fori_loop(1, R, await_cols, 0)
    acc_in.wait()
    for q in range(Q):
        hi, lo = split(cols[q])
        chi[q] = hi
        clo[q] = lo
    feats = cols[0]
    ncol[...] = lax.dot_general(
        jnp.ones((8, F), jnp.float32), feats * feats, (((1,), (1,)), ((), ())),
        precision=lax.Precision.HIGHEST, preferred_element_type=jnp.float32)
    colacc[...] = jnp.zeros_like(colacc)
    tacc[...] = jnp.zeros_like(tacc)

    def shard_of(j):
        out = pick([table[0][i] for i in range(Z)], j)
        for place_z in range(1, Z):
            out = jnp.where(z == place_z, pick([table[place_z][i] for i in range(Z)], j), out)
        return out

    def exchange(zs):
        return remote(rowp.at[at(zs * 2 * NR + (1 - k) * NR, NR, 8), :], sibp.at[zs], rss.at[zs], rsr.at[zs], sibling)

    def out_copy(zs):
        block = at(zs * 2 * NR, 2 * NR, 8)
        return pltpu.make_async_copy(accv.at[block, :], acc_out.at[block, :], osem.at[zs])

    def compute(zs):
        for i in range(n):
            scopy(zs, 1 - k, i).wait_recv()
        block = at(zs * 2 * NR, 2 * NR, 8)
        f = rows[0, block, :]
        cross = lax.dot_general(f, cols[0], (((1,), (1,)), ((), ())), precision=lax.Precision.HIGHEST, preferred_element_type=jnp.float32)
        g = accv[block, :]
        for q in range(1, Q):
            g = g + dot3(split(rows[q, block, :]), (chi[q], clo[q]), 1, 1)
        accv[block, :] = g
        out_copy(zs).start()
        dist = jnp.sum(f * f, axis=1, keepdims=True) + ncol[0:1, :] - 2.0 * cross
        w = g * jnp.exp(-decay_rate * dist)
        s = jnp.sum(w, axis=1, keepdims=True)
        rowp[block, :] = grad_scale * (dot3(split(w), (chi[0], clo[0]), 1, 0) - s * f)
        exchange(zs).start()
        colacc[...] += dot3(split(w.T), split(f), 1, 0)
        tacc[...] += jnp.broadcast_to(jnp.sum(w, axis=0, keepdims=True), tacc.shape)

    def chain_copy(d, zs):
        return remote(sumb.at[zs], chbuf.at[d, zs], chs.at[zs], chrecv.at[d, zs], (me_r, me_c + step_to[d]))

    def chain(zs):
        exchange(zs).wait_recv()
        sumb[zs] = rowp[at(zs * 2 * NR + k * NR, NR, 8), :] + sibp[zs]
        for d in range(2):
            @pl.when(zs > z if d == 0 else zs < z)
            def _():
                @pl.when(place[d] > 0)
                def _():
                    chain_copy(d, zs).wait_recv()
                    sumb[zs] += chbuf[d, zs]

                chain_copy(d, zs).start()

    needs = need + [need[-1]]

    def step(j, carry):
        @pl.when(j > 0)
        def _():
            lax.fori_loop(pick(needs, j - 1), pick(needs, j), slot, 0)

        compute(shard_of(j))

        @pl.when(jnp.logical_and(j > 0, j < Z - 1))
        def _():
            chain(shard_of(j - 1))

        return carry

    lax.fori_loop(0, Z, step, 0)

    def grad_send(p):
        to = (me_r + p) % R
        return remote(colacc.at[at(to * NC, NC, 8), :], colr.at[me_r], gcs.at[p], gcr.at[me_r], (to, me_c))

    def grad_recv(p):
        src = (me_r + p) % R
        return remote(colacc.at[at(src * NC, NC, 8), :], colr.at[src], gcs.at[p], gcr.at[src], (src, me_c))

    tcol = jnp.broadcast_to(tacc[0:1, :], (128, tacc.shape[1])).T[:, 0:1]
    colacc[...] = grad_scale * (colacc[...] - tcol * cols[0])

    def push_grad(p, carry):
        grad_send(p).start()
        return carry

    lax.fori_loop(1, R, push_grad, 0)

    def last_chain(j, carry):
        chain(shard_of(j))
        return carry

    lax.fori_loop(max(Z - 2, 0), Z, last_chain, 0)
    for d in range(2):
        @pl.when(place[d] > 0)
        def _():
            chain_copy(d, z).wait_recv()
            sumb[z] += chbuf[d, z]
    gr_out[...] = sumb[z]

    gc_out[...] = colacc[at(me_r * NC, NC, 8), :]

    def add_grad(p, carry):
        grad_recv(p).wait_recv()
        gc_out[...] += colr[(me_r + p) % R]
        return carry

    lax.fori_loop(1, R, add_grad, 0)

    def drain_peer(p, carry):
        for q in range(Q):
            col_send(p, q).wait_send()
        grad_send(p).wait_send()
        return carry

    lax.fori_loop(1, R, drain_peer, 0)
    for d in range(2):
        y = place[d]

        @pl.when(y < Z - 1)
        def _():
            def drain(ys, carry):
                zs = ys if d == 0 else Z - 1 - ys
                for i in range(n):
                    zcopy(d, zs, i).wait_send()
                return carry

            lax.fori_loop(0, y + 1, drain, 0)

    def drain_shard(zs, carry):
        for i in range(n):
            scopy(zs, k, i).wait_send()
        exchange(zs).wait_send()
        out_copy(zs).wait()

        for d in range(2):
            @pl.when(zs > z if d == 0 else zs < z)
            def _():
                chain_copy(d, zs).wait_send()
        return carry

    lax.fori_loop(0, Z, drain_shard, 0)


def solution(mesh):
    R, C = mesh.shape["row"], mesh.shape["col"]
    in_specs = (
        P(("row", "col"), None),
        P(("col", "row"), None),
        P(("row", "col"), None),
        P(("col", "row"), None),
        P("row", "col"),
    )
    out_specs = (P("row", "col"), P(("row", "col"), None), P(("col", "row"), None))

    def local(fr, fc, pr, pc, acc):
        NR, F = fr.shape
        NC = fc.shape[0]
        Q = 1 + pr.shape[1] // F
        Z, n = C // 2, HALVES * Q
        f32, bf16 = jnp.float32, jnp.bfloat16
        V, D = pltpu.VMEM, pltpu.SemaphoreType.DMA
        hbm = pl.BlockSpec(memory_space=pl.ANY)
        vmem = pl.BlockSpec(memory_space=pltpu.VMEM)
        return pl.pallas_call(
            functools.partial(kernel, R, C),
            out_shape=(
                jax.ShapeDtypeStruct(acc.shape, f32),
                jax.ShapeDtypeStruct(fr.shape, f32),
                jax.ShapeDtypeStruct(fc.shape, f32),
            ),
            in_specs=[hbm] * 5,
            out_specs=(hbm, vmem, vmem),
            scratch_shapes=[
                V((Q, C * NR, F), f32), V((Q, R * NC, F), f32),
                V((Q, R * NC, F), bf16), V((Q, R * NC, F), bf16),
                V((8, R * NC), f32), V(acc.shape, f32),
                V((C * NR, F), f32), V((Z, NR, F), f32), V((2, Z, NR, F), f32), V((Z, NR, F), f32),
                V((R * NC, F), f32), V((8, R * NC), f32), V((R, NC, F), f32),
                D((2 * Q + 1,)), D((Z,)), D((C, n)), D((2, Z, n)), D((Z, n)),
                D((R, Q)), D((R, Q)), D((Z,)), D((Z,)), D((Z,)), D((2, Z)), D((R,)), D((R,)),
            ],
            compiler_params=pltpu.CompilerParams(
                collective_id=0, has_side_effects=True, vmem_limit_bytes=56 * 1024 * 1024),
        )(fr, fc, pr, pc, acc)

    return jax.shard_map(local, mesh=mesh, in_specs=in_specs, out_specs=out_specs, check_vma=False)
```

```python
import functools

import jax
import jax.numpy as jnp
from jax import lax
from jax.experimental import pallas as pl
from jax.experimental.pallas import tpu as pltpu
from jax.sharding import PartitionSpec as P

decay_rate = 0.125
grad_scale = 0.25
MESH = pl.DeviceIdType.MESH
HALVES = 2
LEAD = 3


def split(x):
    hi = x.astype(jnp.bfloat16)
    return hi, (x - hi.astype(jnp.float32)).astype(jnp.bfloat16)


def dot3(a, b, ca, cb):
    dims = (((ca,), (cb,)), ((), ()))
    f = functools.partial(lax.dot_general, dimension_numbers=dims, preferred_element_type=jnp.float32)
    return f(a[0], b[0]) + (f(a[0], b[1]) + f(a[1], b[0]))


def order(n, depth, y, t):
    src, chunk = y * 0, t * 0
    found = y < 0
    for _ in range(depth):
        lead = t < LEAD
        done = jnp.logical_or(lead, t >= LEAD + n * y)
        take = jnp.logical_and(done, jnp.logical_not(found))
        src = jnp.where(take, y, src)
        chunk = jnp.where(take, jnp.where(lead, t, t - n * y), chunk)
        found = jnp.logical_or(found, done)
        y, t = y - 1, t - LEAD
    return src, chunk


def done_slot(n, depth, z, s):
    def seq(y):
        if y == 0:
            return [(0, i) for i in range(n)]
        own = [(y, i) for i in range(n)]
        return own[:LEAD] + seq(y - 1) + own[LEAD:]

    if s == z:
        return -1
    y, ys = (z, s) if s < z else (depth - 1 - z, depth - 1 - s)
    return max(t for t, (a, _) in enumerate(seq(y - 1)) if a == ys)


def plan(n, depth):
    table, need = [], [0] * depth
    for z in range(depth):
        shards = sorted(range(depth), key=lambda s: (done_slot(n, depth, z, s), -abs(s - z)))
        far = [s for s in shards if s != z]
        if z in (0, depth - 1):
            far.insert(len(far) - 1, z)
        else:
            far = sorted(far, key=lambda s: (-abs(s - z), s < z)) + [z]
        table.append(far)
        for j, s in enumerate(far):
            need[j] = max(need[j], done_slot(n, depth, z, s) + 1)
    for j in range(1, depth):
        need[j] = max(need[j], need[j - 1])
    need[0] = max(need[0], n * (depth - 2))
    for j in range(1, depth):
        need[j] = max(need[j], need[0])
    need[-1] = max(need[-1], n * (depth - 1))
    return table, need


def pick(values, at):
    out = jnp.int32(values[0])
    for i, v in enumerate(values[1:], 1):
        out = jnp.where(at == i, jnp.int32(v), out)
    return out


def kernel(R, C, fr, fc, pr, pc, acc, accv, gr_out, gc_out,
           rows, cols, chi, clo, ncol, rowp, sibp, chbuf, sumb, colacc, tacc, colr,
           lsem, rrecv, zss, sss, css, crecv, rss, rsr, chs, chrecv, gcs, gcr):
    me_r, me_c = lax.axis_index("row"), lax.axis_index("col")
    z, k = me_c // 2, me_c % 2
    Z = C // 2
    NR, F = fr.shape
    NC = fc.shape[0]
    Q = 1 + pr.shape[1] // F
    n = HALVES * Q
    hr = NR // HALVES
    sibling = (me_r, me_c + 1 - 2 * k)
    place = (z, Z - 1 - z)
    step_to = (2, -2)
    table, need = plan(n, Z)

    def at(start, size, mult):
        return pl.ds(pl.multiple_of(start, mult), size)

    def rchunk(c, i):
        return rows.at[i % Q, at(c * NR + (i // Q) * hr, hr, 8), :]

    def remote(src, dst, ss, rs, dev):
        return pltpu.make_async_remote_copy(src_ref=src, dst_ref=dst, send_sem=ss, recv_sem=rs, device_id=dev, device_id_type=MESH)

    def zcopy(d, zs, i):
        c = 2 * zs + k
        return remote(rchunk(c, i), rchunk(c, i), zss.at[d, zs, i], rrecv.at[c, i], (me_r, me_c + step_to[d]))

    def scopy(zs, core, i):
        c = 2 * zs + core
        return remote(rchunk(c, i), rchunk(c, i), sss.at[zs, i], rrecv.at[c, i], sibling)

    local = []
    for q in range(Q):
        rsrc = fr if q == 0 else pr.at[:, pl.ds((q - 1) * F, F)]
        csrc = fc if q == 0 else pc.at[:, pl.ds((q - 1) * F, F)]
        local.append(pltpu.make_async_copy(rsrc, rows.at[q, at(me_c * NR, NR, 8), :], lsem.at[2 * q]))
        local.append(pltpu.make_async_copy(csrc, cols.at[q, at(me_r * NC, NC, 8), :], lsem.at[2 * q + 1]))
    acc_in = pltpu.make_async_copy(acc, accv, lsem.at[2 * Q])
    for copy in local:
        copy.start()
    acc_in.start()

    barrier = pltpu.get_barrier_semaphore()

    def greet(p, carry):
        pl.semaphore_signal(barrier, inc=1, device_id=((me_r + p) % R, me_c), device_id_type=MESH)
        return carry

    lax.fori_loop(1, R, greet, 0)
    pl.semaphore_signal(barrier, inc=1, device_id=sibling, device_id_type=MESH)
    for d in range(2):
        @pl.when(place[d] < Z - 1)
        def _():
            pl.semaphore_signal(barrier, inc=1, device_id=(me_r, me_c + step_to[d]), device_id_type=MESH)
    for copy in local:
        copy.wait()
    pl.semaphore_wait(barrier, R + (z > 0).astype(jnp.int32) + (z < Z - 1).astype(jnp.int32))

    for d in range(2):
        @pl.when(place[d] < Z - 1)
        def _():
            for i in range(LEAD):
                zcopy(d, z, i).start()

    def col_send(p, q):
        block = cols.at[q, at(me_r * NC, NC, 8), :]
        return remote(block, block, css.at[p, q], crecv.at[me_r, q], ((me_r + p) % R, me_c))

    def col_recv(p, q):
        src = (me_r + p) % R
        block = cols.at[q, at(src * NC, NC, 8), :]
        return remote(block, block, css.at[p, q], crecv.at[src, q], ((me_r + p) % R, me_c))

    def push_cols(p, carry):
        for q in range(Q):
            col_send(p, q).start()
        return carry

    lax.fori_loop(1, R, push_cols, 0)
    for d in range(2):
        @pl.when(place[d] == 0)
        def _():
            for i in range(LEAD, n):
                zcopy(d, z, i).start()
    for i in range(n):
        scopy(z, k, i).start()

    def slot(t, carry):
        for d in range(2):
            y = place[d]

            @pl.when(t < n * y)
            def _():
                ys, i = order(n, Z, y - 1, t)
                zs = ys if d == 0 else Z - 1 - ys
                zcopy(d, zs, i).wait_recv()

                @pl.when(y < Z - 1)
                def _():
                    zcopy(d, zs, i).start()

                scopy(zs, k, i).start()

                @pl.when(jnp.logical_and(t == n * y - 1, y < Z - 1))
                def _():
                    for j in range(LEAD, n):
                        zcopy(d, z, j).start()

        return carry

    lax.fori_loop(0, need[0], slot, 0)

    def await_cols(p, carry):
        for q in range(Q):
            col_recv(p, q).wait_recv()
        return carry

    lax.fori_loop(1, R, await_cols, 0)
    acc_in.wait()
    for q in range(Q):
        hi, lo = split(cols[q])
        chi[q] = hi
        clo[q] = lo
    feats = cols[0]
    ncol[...] = lax.dot_general(
        jnp.ones((8, F), jnp.float32), feats * feats, (((1,), (1,)), ((), ())),
        precision=lax.Precision.HIGHEST, preferred_element_type=jnp.float32)
    colacc[...] = jnp.zeros_like(colacc)
    tacc[...] = jnp.zeros_like(tacc)

    def shard_of(j):
        out = pick([table[0][i] for i in range(Z)], j)
        for place_z in range(1, Z):
            out = jnp.where(z == place_z, pick([table[place_z][i] for i in range(Z)], j), out)
        return out

    def exchange(zs):
        return remote(rowp.at[at(zs * 2 * NR + (1 - k) * NR, NR, 8), :], sibp.at[zs], rss.at[zs], rsr.at[zs], sibling)

    def compute(zs):
        for i in range(n):
            scopy(zs, 1 - k, i).wait_recv()
        block = at(zs * 2 * NR, 2 * NR, 8)
        f = rows[0, block, :]
        cross = lax.dot_general(f, cols[0], (((1,), (1,)), ((), ())), precision=lax.Precision.HIGHEST, preferred_element_type=jnp.float32)
        g = accv[block, :]
        for q in range(1, Q):
            g = g + dot3(split(rows[q, block, :]), (chi[q], clo[q]), 1, 1)
        accv[block, :] = g
        dist = jnp.sum(f * f, axis=1, keepdims=True) + ncol[0:1, :] - 2.0 * cross
        w = g * jnp.exp(-decay_rate * dist)
        s = jnp.sum(w, axis=1, keepdims=True)
        rowp[block, :] = grad_scale * (dot3(split(w), (chi[0], clo[0]), 1, 0) - s * f)
        exchange(zs).start()
        colacc[...] += dot3(split(w.T), split(f), 1, 0)
        tacc[...] += jnp.broadcast_to(jnp.sum(w, axis=0, keepdims=True), tacc.shape)

    def chain_copy(d, zs):
        return remote(sumb.at[zs], chbuf.at[d, zs], chs.at[zs], chrecv.at[d, zs], (me_r, me_c + step_to[d]))

    def chain(zs):
        exchange(zs).wait_recv()
        sumb[zs] = rowp[at(zs * 2 * NR + k * NR, NR, 8), :] + sibp[zs]
        for d in range(2):
            @pl.when(zs > z if d == 0 else zs < z)
            def _():
                @pl.when(place[d] > 0)
                def _():
                    chain_copy(d, zs).wait_recv()
                    sumb[zs] += chbuf[d, zs]

                chain_copy(d, zs).start()

    needs = need + [need[-1]]

    def step(j, carry):
        @pl.when(j > 0)
        def _():
            lax.fori_loop(pick(needs, j - 1), pick(needs, j), slot, 0)

        compute(shard_of(j))

        @pl.when(jnp.logical_and(j > 0, j < Z - 1))
        def _():
            chain(shard_of(j - 1))

        return carry

    lax.fori_loop(0, Z, step, 0)

    def grad_send(p):
        to = (me_r + p) % R
        return remote(colacc.at[at(to * NC, NC, 8), :], colr.at[me_r], gcs.at[p], gcr.at[me_r], (to, me_c))

    def grad_recv(p):
        src = (me_r + p) % R
        return remote(colacc.at[at(src * NC, NC, 8), :], colr.at[src], gcs.at[p], gcr.at[src], (src, me_c))

    tcol = jnp.broadcast_to(tacc[0:1, :], (128, tacc.shape[1])).T[:, 0:1]
    colacc[...] = grad_scale * (colacc[...] - tcol * cols[0])

    def push_grad(p, carry):
        grad_send(p).start()
        return carry

    lax.fori_loop(1, R, push_grad, 0)

    def last_chain(j, carry):
        chain(shard_of(j))
        return carry

    lax.fori_loop(max(Z - 2, 0), Z, last_chain, 0)
    for d in range(2):
        @pl.when(place[d] > 0)
        def _():
            chain_copy(d, z).wait_recv()
            sumb[z] += chbuf[d, z]
    gr_out[...] = sumb[z]

    gc_out[...] = colacc[at(me_r * NC, NC, 8), :]

    def add_grad(p, carry):
        grad_recv(p).wait_recv()
        gc_out[...] += colr[(me_r + p) % R]
        return carry

    lax.fori_loop(1, R, add_grad, 0)

    def drain_peer(p, carry):
        for q in range(Q):
            col_send(p, q).wait_send()
        grad_send(p).wait_send()
        return carry

    lax.fori_loop(1, R, drain_peer, 0)
    for d in range(2):
        y = place[d]

        @pl.when(y < Z - 1)
        def _():
            def drain(ys, carry):
                zs = ys if d == 0 else Z - 1 - ys
                for i in range(n):
                    zcopy(d, zs, i).wait_send()
                return carry

            lax.fori_loop(0, y + 1, drain, 0)

    def drain_shard(zs, carry):
        for i in range(n):
            scopy(zs, k, i).wait_send()
        exchange(zs).wait_send()

        for d in range(2):
            @pl.when(zs > z if d == 0 else zs < z)
            def _():
                chain_copy(d, zs).wait_send()
        return carry

    lax.fori_loop(0, Z, drain_shard, 0)


def solution(mesh):
    R, C = mesh.shape["row"], mesh.shape["col"]
    in_specs = (
        P(("row", "col"), None),
        P(("col", "row"), None),
        P(("row", "col"), None),
        P(("col", "row"), None),
        P("row", "col"),
    )
    out_specs = (P("row", "col"), P(("row", "col"), None), P(("col", "row"), None))

    def local(fr, fc, pr, pc, acc):
        NR, F = fr.shape
        NC = fc.shape[0]
        Q = 1 + pr.shape[1] // F
        Z, n = C // 2, HALVES * Q
        f32, bf16 = jnp.float32, jnp.bfloat16
        V, D = pltpu.VMEM, pltpu.SemaphoreType.DMA
        hbm = pl.BlockSpec(memory_space=pl.ANY)
        vmem = pl.BlockSpec(memory_space=pltpu.VMEM)
        shapes = (acc.shape, fr.shape, fc.shape)
        made = pl.pallas_call(
            functools.partial(kernel, R, C),
            out_shape=tuple(pltpu.VMEM(s, f32) for s in shapes),
            in_specs=[hbm] * 5,
            out_specs=(vmem,) * 3,
            scratch_shapes=[
                V((Q, C * NR, F), f32), V((Q, R * NC, F), f32),
                V((Q, R * NC, F), bf16), V((Q, R * NC, F), bf16),
                V((8, R * NC), f32),
                V((C * NR, F), f32), V((Z, NR, F), f32), V((2, Z, NR, F), f32), V((Z, NR, F), f32),
                V((R * NC, F), f32), V((8, R * NC), f32), V((R, NC, F), f32),
                D((2 * Q + 1,)), D((C, n)), D((2, Z, n)), D((Z, n)),
                D((R, Q)), D((R, Q)), D((Z,)), D((Z,)), D((Z,)), D((2, Z)), D((R,)), D((R,)),
            ],
            compiler_params=pltpu.CompilerParams(
                collective_id=0, has_side_effects=True, vmem_limit_bytes=56 * 1024 * 1024),
        )(fr, fc, pr, pc, acc)
        return tuple(made)

    return jax.shard_map(local, mesh=mesh, in_specs=in_specs, out_specs=out_specs, check_vma=False)
```

```python
import functools

import jax
import jax.numpy as jnp
from jax import lax
from jax.experimental import pallas as pl
from jax.experimental.pallas import tpu as pltpu
from jax.sharding import PartitionSpec as P

decay_rate = 0.125
grad_scale = 0.25
MESH = pl.DeviceIdType.MESH
HALVES = 2
LEAD = 3
RELAY_SLOTS = 2


def split(x):
    hi = x.astype(jnp.bfloat16)
    return hi, (x - hi.astype(jnp.float32)).astype(jnp.bfloat16)


def dot3(a, b, ca, cb):
    dims = (((ca,), (cb,)), ((), ()))
    f = functools.partial(lax.dot_general, dimension_numbers=dims, preferred_element_type=jnp.float32)
    return f(a[0], b[0]) + (f(a[0], b[1]) + f(a[1], b[0]))


def order(n, depth, y, t):
    src, chunk = y * 0, t * 0
    found = y < 0
    for _ in range(depth):
        lead = t < LEAD
        done = jnp.logical_or(lead, t >= LEAD + n * y)
        take = jnp.logical_and(done, jnp.logical_not(found))
        src = jnp.where(take, y, src)
        chunk = jnp.where(take, jnp.where(lead, t, t - n * y), chunk)
        found = jnp.logical_or(found, done)
        y, t = y - 1, t - LEAD
    return src, chunk


def done_slot(n, depth, z, s):
    def seq(y):
        if y == 0:
            return [(0, i) for i in range(n)]
        own = [(y, i) for i in range(n)]
        return own[:LEAD] + seq(y - 1) + own[LEAD:]

    if s == z:
        return -1
    y, ys = (z, s) if s < z else (depth - 1 - z, depth - 1 - s)
    return max(t for t, (a, _) in enumerate(seq(y - 1)) if a == ys)


def plan(n, depth):
    table, need = [], [0] * depth
    for z in range(depth):
        shards = sorted(range(depth), key=lambda s: (done_slot(n, depth, z, s), -abs(s - z)))
        far = [s for s in shards if s != z]
        if z in (0, depth - 1):
            far.insert(len(far) - 1, z)
        else:
            far = sorted(far, key=lambda s: 2 * z + depth - 1 - s if s > z else 2 * (depth - 1 - z) + s) + [z]
        table.append(far)
        for j, s in enumerate(far):
            need[j] = max(need[j], done_slot(n, depth, z, s) + 1)
    for j in range(1, depth):
        need[j] = max(need[j], need[j - 1])
    need[0] = max(need[0], n * (depth - 2))
    for j in range(1, depth):
        need[j] = max(need[j], need[0])
    need[-1] = max(need[-1], n * (depth - 1))
    return table, need


def pick(values, at):
    out = jnp.int32(values[0])
    for i, v in enumerate(values[1:], 1):
        out = jnp.where(at == i, jnp.int32(v), out)
    return out


def kernel(R, C, fr, fc, pr, pc, acc, accv, gr_out, gc_out,
           rows, cols, chi, clo, ncol, rowp, sibp, chbuf, sumb, colacc, tacc, colr,
           lsem, rrecv, zss, sss, css, crecv, rss, rsr, chs, chrecv, gcs, gcr, ys, yr):
    me_r, me_c = lax.axis_index("row"), lax.axis_index("col")
    z, k = me_c // 2, me_c % 2
    Z = C // 2
    NR, F = fr.shape
    NC = fc.shape[0]
    Q = 1 + pr.shape[1] // F
    n = HALVES * Q
    hr = NR // HALVES
    sibling = (me_r, me_c + 1 - 2 * k)
    place = (z, Z - 1 - z)
    step_to = (2, -2)
    table, need = plan(n, Z)

    def at(start, size, mult):
        return pl.ds(pl.multiple_of(start, mult), size)

    def rchunk(c, i):
        return rows.at[i % Q, at(c * NR + (i // Q) * hr, hr, 8), :]

    def remote(src, dst, ss, rs, dev):
        return pltpu.make_async_remote_copy(src_ref=src, dst_ref=dst, send_sem=ss, recv_sem=rs, device_id=dev, device_id_type=MESH)

    def zcopy(d, zs, i):
        c = 2 * zs + k
        return remote(rchunk(c, i), rchunk(c, i), zss.at[d, zs, i], rrecv.at[c, i], (me_r, me_c + step_to[d]))

    def scopy(zs, core, i):
        c = 2 * zs + core
        return remote(rchunk(c, i), rchunk(c, i), sss.at[zs, i], rrecv.at[c, i], sibling)

    local = []
    for q in range(Q):
        rsrc = fr if q == 0 else pr.at[:, pl.ds((q - 1) * F, F)]
        csrc = fc if q == 0 else pc.at[:, pl.ds((q - 1) * F, F)]
        local.append(pltpu.make_async_copy(rsrc, rows.at[q, at(me_c * NR, NR, 8), :], lsem.at[2 * q]))
        local.append(pltpu.make_async_copy(csrc, cols.at[q, at(me_r * NC, NC, 8), :], lsem.at[2 * q + 1]))
    acc_in = pltpu.make_async_copy(acc, accv, lsem.at[2 * Q])
    for copy in local:
        copy.start()
    acc_in.start()

    barrier = pltpu.get_barrier_semaphore()

    def greet(p, carry):
        pl.semaphore_signal(barrier, inc=1, device_id=((me_r + p) % R, me_c), device_id_type=MESH)
        return carry

    lax.fori_loop(1, R, greet, 0)
    pl.semaphore_signal(barrier, inc=1, device_id=sibling, device_id_type=MESH)
    for d in range(2):
        @pl.when(place[d] < Z - 1)
        def _():
            pl.semaphore_signal(barrier, inc=1, device_id=(me_r, me_c + step_to[d]), device_id_type=MESH)
    for copy in local:
        copy.wait()
    pl.semaphore_wait(barrier, R + (z > 0).astype(jnp.int32) + (z < Z - 1).astype(jnp.int32))

    for d in range(2):
        @pl.when(place[d] < Z - 1)
        def _():
            for i in range(LEAD):
                zcopy(d, z, i).start()

    def col_send(p, q):
        block = cols.at[q, at(me_r * NC, NC, 8), :]
        return remote(block, block, css.at[p, q], crecv.at[me_r, q], ((me_r + p) % R, me_c))

    def col_recv(p, q):
        src = (me_r + p) % R
        block = cols.at[q, at(src * NC, NC, 8), :]
        return remote(block, block, css.at[p, q], crecv.at[src, q], ((me_r + p) % R, me_c))

    def push_cols(p, carry):
        for q in range(Q):
            col_send(p, q).start()
        return carry

    square = R == 4
    near = (me_r // 2 * 2 + 1 - me_r % 2, (1 - me_r // 2) * 2 + me_r % 2)
    across = R - 1 - me_r

    def own_push(axis, q):
        block = cols.at[q, at(me_r * NC, NC, 8), :]
        return remote(block, block, css.at[axis, q], crecv.at[me_r, q], (near[axis], me_c))

    def own_arrive(axis, q):
        block = cols.at[q, at(near[axis] * NC, NC, 8), :]
        return remote(block, block, css.at[axis, q], crecv.at[near[axis], q], (near[axis], me_c))

    def relay(axis, q, owner):
        block = cols.at[q, at(owner * NC + axis * (NC // 2), NC // 2, 8), :]
        return remote(block, block, ys.at[axis, q], yr.at[axis, q], (near[1 - axis], me_c))

    if square:
        for q in range(Q):
            for axis in range(2):
                own_push(axis, q).start()
    else:
        lax.fori_loop(1, R, push_cols, 0)
    for d in range(2):
        @pl.when(place[d] == 0)
        def _():
            for i in range(LEAD, n):
                zcopy(d, z, i).start()
    for i in range(n):
        scopy(z, k, i).start()

    def slot(t, carry):
        for d in range(2):
            y = place[d]

            @pl.when(t < n * y)
            def _():
                ys, i = order(n, Z, y - 1, t)
                zs = ys if d == 0 else Z - 1 - ys
                zcopy(d, zs, i).wait_recv()

                @pl.when(y < Z - 1)
                def _():
                    zcopy(d, zs, i).start()

                scopy(zs, k, i).start()

                @pl.when(jnp.logical_and(t == n * y - 1, y < Z - 1))
                def _():
                    for j in range(LEAD, n):
                        zcopy(d, z, j).start()

        return carry

    passed = 0
    if square:
        for q in range(Q):
            upto = min(RELAY_SLOTS * (q + 1), need[0])
            lax.fori_loop(passed, upto, slot, 0)
            passed = upto
            for axis in range(2):
                own_arrive(axis, q).wait_recv()
                relay(axis, q, near[axis]).start()
    lax.fori_loop(passed, need[0], slot, 0)

    def await_cols(p, carry):
        for q in range(Q):
            col_recv(p, q).wait_recv()
        return carry

    if square:
        for q in range(Q):
            for axis in range(2):
                relay(axis, q, across).wait_recv()
    else:
        lax.fori_loop(1, R, await_cols, 0)
    acc_in.wait()
    for q in range(Q):
        hi, lo = split(cols[q])
        chi[q] = hi
        clo[q] = lo
    feats = cols[0]
    ncol[...] = lax.dot_general(
        jnp.ones((8, F), jnp.float32), feats * feats, (((1,), (1,)), ((), ())),
        precision=lax.Precision.HIGHEST, preferred_element_type=jnp.float32)
    colacc[...] = jnp.zeros_like(colacc)
    tacc[...] = jnp.zeros_like(tacc)

    def shard_of(j):
        out = pick([table[0][i] for i in range(Z)], j)
        for place_z in range(1, Z):
            out = jnp.where(z == place_z, pick([table[place_z][i] for i in range(Z)], j), out)
        return out

    def exchange(zs):
        return remote(rowp.at[at(zs * 2 * NR + (1 - k) * NR, NR, 8), :], sibp.at[zs], rss.at[zs], rsr.at[zs], sibling)

    def compute(zs):
        for i in range(n):
            scopy(zs, 1 - k, i).wait_recv()
        block = at(zs * 2 * NR, 2 * NR, 8)
        f = rows[0, block, :]
        cross = lax.dot_general(f, cols[0], (((1,), (1,)), ((), ())), precision=lax.Precision.HIGHEST, preferred_element_type=jnp.float32)
        g = accv[block, :]
        for q in range(1, Q):
            g = g + dot3(split(rows[q, block, :]), (chi[q], clo[q]), 1, 1)
        accv[block, :] = g
        dist = jnp.sum(f * f, axis=1, keepdims=True) + ncol[0:1, :] - 2.0 * cross
        w = g * jnp.exp(-decay_rate * dist)
        s = jnp.sum(w, axis=1, keepdims=True)
        rowp[block, :] = grad_scale * (dot3(split(w), (chi[0], clo[0]), 1, 0) - s * f)
        exchange(zs).start()
        colacc[...] += dot3(split(w.T), split(f), 1, 0)
        tacc[...] += jnp.broadcast_to(jnp.sum(w, axis=0, keepdims=True), tacc.shape)

    def chain_copy(d, zs):
        return remote(sumb.at[zs], chbuf.at[d, zs], chs.at[zs], chrecv.at[d, zs], (me_r, me_c + step_to[d]))

    def chain(zs):
        exchange(zs).wait_recv()
        sumb[zs] = rowp[at(zs * 2 * NR + k * NR, NR, 8), :] + sibp[zs]
        for d in range(2):
            @pl.when(zs > z if d == 0 else zs < z)
            def _():
                @pl.when(place[d] > 0)
                def _():
                    chain_copy(d, zs).wait_recv()
                    sumb[zs] += chbuf[d, zs]

                chain_copy(d, zs).start()

    needs = need + [need[-1]]
    at_end = jnp.logical_or(z == 0, z == Z - 1)

    def step(j, carry):
        @pl.when(j > 0)
        def _():
            lax.fori_loop(pick(needs, j - 1), pick(needs, j), slot, 0)

        compute(shard_of(j))

        @pl.when(jnp.logical_and(at_end, j < Z - 2))
        def _():
            chain(shard_of(j))

        return carry

    lax.fori_loop(0, Z, step, 0)

    def grad_send(p):
        to = (me_r + p) % R
        return remote(colacc.at[at(to * NC, NC, 8), :], colr.at[me_r], gcs.at[p], gcr.at[me_r], (to, me_c))

    def grad_recv(p):
        src = (me_r + p) % R
        return remote(colacc.at[at(src * NC, NC, 8), :], colr.at[src], gcs.at[p], gcr.at[src], (src, me_c))

    tcol = jnp.broadcast_to(tacc[0:1, :], (128, tacc.shape[1])).T[:, 0:1]
    colacc[...] = grad_scale * (colacc[...] - tcol * cols[0])

    def push_grad(p, carry):
        grad_send(p).start()
        return carry

    lax.fori_loop(1, R, push_grad, 0)

    def last_chain(j, carry):
        chain(shard_of(j))
        return carry

    lax.fori_loop(jnp.where(at_end, max(Z - 2, 0), 0), Z, last_chain, 0)
    for d in range(2):
        @pl.when(place[d] > 0)
        def _():
            chain_copy(d, z).wait_recv()
            sumb[z] += chbuf[d, z]
    gr_out[...] = sumb[z]

    gc_out[...] = colacc[at(me_r * NC, NC, 8), :]

    def add_grad(p, carry):
        grad_recv(p).wait_recv()
        gc_out[...] += colr[(me_r + p) % R]
        return carry

    lax.fori_loop(1, R, add_grad, 0)

    def drain_peer(p, carry):
        if not square:
            for q in range(Q):
                col_send(p, q).wait_send()
        grad_send(p).wait_send()
        return carry

    lax.fori_loop(1, R, drain_peer, 0)
    if square:
        for q in range(Q):
            for axis in range(2):
                own_push(axis, q).wait_send()
                relay(axis, q, near[axis]).wait_send()
    for d in range(2):
        y = place[d]

        @pl.when(y < Z - 1)
        def _():
            def drain(ys, carry):
                zs = ys if d == 0 else Z - 1 - ys
                for i in range(n):
                    zcopy(d, zs, i).wait_send()
                return carry

            lax.fori_loop(0, y + 1, drain, 0)

    def drain_shard(zs, carry):
        for i in range(n):
            scopy(zs, k, i).wait_send()
        exchange(zs).wait_send()

        for d in range(2):
            @pl.when(zs > z if d == 0 else zs < z)
            def _():
                chain_copy(d, zs).wait_send()
        return carry

    lax.fori_loop(0, Z, drain_shard, 0)


def solution(mesh):
    R, C = mesh.shape["row"], mesh.shape["col"]
    in_specs = (
        P(("row", "col"), None),
        P(("col", "row"), None),
        P(("row", "col"), None),
        P(("col", "row"), None),
        P("row", "col"),
    )
    out_specs = (P("row", "col"), P(("row", "col"), None), P(("col", "row"), None))

    def local(fr, fc, pr, pc, acc):
        NR, F = fr.shape
        NC = fc.shape[0]
        Q = 1 + pr.shape[1] // F
        Z, n = C // 2, HALVES * Q
        f32, bf16 = jnp.float32, jnp.bfloat16
        V, D = pltpu.VMEM, pltpu.SemaphoreType.DMA
        hbm = pl.BlockSpec(memory_space=pl.ANY)
        vmem = pl.BlockSpec(memory_space=pltpu.VMEM)
        shapes = (acc.shape, fr.shape, fc.shape)
        made = pl.pallas_call(
            functools.partial(kernel, R, C),
            out_shape=tuple(pltpu.VMEM(s, f32) for s in shapes),
            in_specs=[hbm] * 5,
            out_specs=(vmem,) * 3,
            scratch_shapes=[
                V((Q, C * NR, F), f32), V((Q, R * NC, F), f32),
                V((Q, R * NC, F), bf16), V((Q, R * NC, F), bf16),
                V((8, R * NC), f32),
                V((C * NR, F), f32), V((Z, NR, F), f32), V((2, Z, NR, F), f32), V((Z, NR, F), f32),
                V((R * NC, F), f32), V((8, R * NC), f32), V((R, NC, F), f32),
                D((2 * Q + 1,)), D((C, n)), D((2, Z, n)), D((Z, n)),
                D((R, Q)), D((R, Q)), D((Z,)), D((Z,)), D((Z,)), D((2, Z)), D((R,)), D((R,)), D((2, Q)), D((2, Q)),
            ],
            compiler_params=pltpu.CompilerParams(
                collective_id=0, has_side_effects=True, vmem_limit_bytes=56 * 1024 * 1024),
        )(fr, fc, pr, pc, acc)
        return tuple(made)

    return jax.shard_map(local, mesh=mesh, in_specs=in_specs, out_specs=out_specs, check_vma=False)
```
